32 devices in a mesh: groups: 2 (over x), rows: 16 (over z, y, core).
Axes of the slice: x: 2, y: 2, z: 4, core: 2. Of those that a mesh axis runs over, the one named last changes fastest.
Arguments:
- orbitals: float32 [32768, 1024], P('rows', 'groups'), parts along dimension 1, may hold values from -6 to 6
- trial_orbitals: float32 [32768, 1024], P('rows', 'groups'), parts along dimension 1, may hold values from -0.03125 to 0.03125
- angles: float32 [128], replicated, may hold values from -3.140625 to 3.140625
- horizontal_index: int32 [4, 64, 512], P('groups', 'rows'), parts along dimension 0, may hold values from 0 to 127
- horizontal_mask: int32 [4, 64, 512], P('groups', 'rows'), parts along dimension 0, may hold values 0 or 1
- vertical_index: int32 [8, 64, 512], P('groups', 'rows'), parts along dimension 0, may hold values from 0 to 127
- vertical_mask: int32 [8, 64, 512], P('groups', 'rows'), parts along dimension 0, may hold values 0 or 1
Outputs:
- evolved: float32 [32768, 1024], P('rows', 'groups'), parts along dimension 1
- intersection: float32 [1024, 512], P('groups'), parts along dimension 0
The draws below stay inside these ranges and needn't reach their ends.
There are 2 independent parts, one for each index of `groups`. The reference program is written for one: setup_inputs(seed, part) draws one part's arguments, and reference() takes and returns one part's arrays. A program takes and returns all parts, laid end to end along the dimension named above; an argument that names none is the same for every part. Nothing has to cross between parts.
All inputs are finite; a program needn't handle non-finite values. No bound on the sum of `horizontal_mask` or of `vertical_mask` on one device may be relied on, other than what follows from the above.
Results may differ from the reference program's by a relative error of at most 0.00012.
Values sent between devices are 32-bit elements; how exact they have to be, the bound alone decides.
No kernel may reach another device: no remote copies, remote signals or barrier semaphores. Data moves between devices by JAX's collectives and lax.ppermute only.
A program may use at most 128 MiB of HBM per device.

```python
import jax
import jax.numpy as jnp
from jax import lax

LX = 512
COLS = 512
NH = 2
NV = 4
NANG = 128
LY = 64
M = 32768


def set_ends(drawn, rng, least, top_value):
    extent = drawn.shape
    place = [jax.random.randint(jax.random.fold_in(rng, axis), (), 0, extent[axis]) for axis in range(len(extent))]
    drawn = drawn.at[tuple(place)].set(least)
    longest = extent.index(max(extent))
    place[longest] = (place[longest] + 1) % extent[longest]
    return drawn.at[tuple(place)].set(top_value)


def block_levels(rng, shape, shards, least, high):
    level, own = 1.0, jax.random.fold_in(rng, 6)
    for position, blocks in shards:
        heights = jnp.exp(jax.random.uniform(jax.random.fold_in(own, position), (blocks,), jnp.float32, least / len(shards), high / len(shards)))
        level = level * jnp.repeat(heights, shape[position] // blocks).reshape([-1 if axis == position else 1 for axis in range(len(shape))])
    return level


def noise(rng, extent, width, reach, shards=(), held_as=jnp.bfloat16):
    level = block_levels(rng, extent, shards, -0.22, 0.18) if shards else 1.0
    values = jax.random.normal(rng, extent, jnp.float32) * width * level
    return jnp.minimum(jnp.maximum(values, -reach), reach).astype(held_as)


def setup_inputs(seed: int = 0, part: int = 0) -> dict:
    streams_of = jax.random.split(jax.random.key(seed), 8)
    part_keys = jax.random.split(jax.random.fold_in(streams_of[7], part), 8)
    orbitals = noise(part_keys[0], (M, COLS), 1.0, 6.0, ((0, 16),), jnp.float32)
    trial_orbitals = noise(part_keys[1], (M, COLS), (LY * LX) ** -0.5, 0.03125, ((0, 16),), jnp.float32)
    angles = jnp.clip(jax.random.uniform(streams_of[2], (NANG,), jnp.float32, -3.140625, 3.140625), -3.140625, 3.140625)
    horizontal_index = set_ends(jax.random.randint(part_keys[3], (NH, LY, LX), 0, NANG), jax.random.fold_in(part_keys[3], 1), 0, NANG - 1).astype(jnp.int32)
    horizontal_mask = set_ends((jax.random.randint(part_keys[4], (NH, LY, LX), 0, 4) < 3).astype(jnp.int32), jax.random.fold_in(part_keys[4], 1), 0, 1)
    vertical_index = set_ends(jax.random.randint(part_keys[5], (NV, LY, LX), 0, NANG), jax.random.fold_in(part_keys[5], 1), 0, NANG - 1).astype(jnp.int32)
    vertical_mask = set_ends((jax.random.randint(part_keys[6], (NV, LY, LX), 0, 4) < 3).astype(jnp.int32), jax.random.fold_in(part_keys[6], 1), 0, 1)
    return {"orbitals": orbitals, "trial_orbitals": trial_orbitals, "angles": angles, "horizontal_index": horizontal_index, "horizontal_mask": horizontal_mask, "vertical_index": vertical_index, "vertical_mask": vertical_mask}


def coefficients(index, mask, cos_table, sin_table):
    active = mask == 1
    return jnp.where(active, cos_table[index], 1.0), jnp.where(active, sin_table[index], 0.0)


def rotate(first_row, second_row, cosine_part, sine_part):
    cosine_part = cosine_part[..., None]
    sine_part = sine_part[..., None]
    return cosine_part * first_row - sine_part * second_row, sine_part * first_row + cosine_part * second_row


def horizontal_even(current, cosine_part, sine_part):
    first_new, second_new = rotate(current[:, 0::2], current[:, 1::2], cosine_part[:, 0::2], sine_part[:, 0::2])
    return jnp.stack([first_new, second_new], axis=2).reshape(current.shape)


def horizontal(current, cosine_part, sine_part, parity):
    if parity == 0:
        return horizontal_even(current, cosine_part, sine_part)
    interior = horizontal_even(current[:, 1:-1], cosine_part[:, 1:-1], sine_part[:, 1:-1])
    return jnp.concatenate([current[:, :1], interior, current[:, -1:]], axis=1)


def vertical_even(current, cosine_part, sine_part):
    lower_new, partner_new = rotate(current[0::2], jnp.flip(current[1::2], axis=1), cosine_part[0::2], sine_part[0::2])
    upper_new = jnp.flip(partner_new, axis=1)
    return jnp.stack([lower_new, upper_new], axis=1).reshape(current.shape)


def reference(orbitals, trial_orbitals, angles, horizontal_index, horizontal_mask, vertical_index, vertical_mask):
    cos_table = jnp.cos(angles)
    sin_table = jnp.sin(angles)
    across_cos, across_sin = coefficients(horizontal_index, horizontal_mask, cos_table, sin_table)
    upward_cos, upward_sin = coefficients(vertical_index, vertical_mask, cos_table, sin_table)
    current = orbitals.reshape(LY, LX, COLS)
    for layer_index in range(NH):
        current = horizontal(current, across_cos[layer_index], across_sin[layer_index], layer_index % 2)
    for layer_index in range(NV):
        if layer_index % 2 == 0:
            current = vertical_even(current, upward_cos[layer_index], upward_sin[layer_index])
        else:
            rolled = vertical_even(jnp.roll(current, -1, 0), jnp.roll(upward_cos[layer_index], -1, 0), jnp.roll(upward_sin[layer_index], -1, 0))
            current = jnp.roll(rolled, 1, 0)
    evolved = current.reshape(LY * LX, COLS)
    intersection = lax.dot_general(trial_orbitals, evolved, (((0,), (0,)), ((), ())), precision=lax.Precision.HIGHEST, preferred_element_type=jnp.float32)
    return evolved, intersection
```

```python
import functools

import jax
import jax.numpy as jnp
from jax import lax
from jax.experimental import pallas as pl
from jax.experimental.pallas import tpu as pltpu
from jax.sharding import PartitionSpec as P

LANES = 128
SUBLANES = 8
BLOCK = 64
ROWS = 4
LAYERS_UP = 4


def own(name):
    return (name + "_cos", name + "_sin")


def lookup(index, mask, table):
    parts = []
    for start in range(0, index.shape[1], LANES):
        piece = index[:, start : start + LANES]
        parts.append(jnp.take_along_axis(table, piece, axis=1, mode="promise_in_bounds"))
    return jnp.concatenate(parts, axis=1)


def coefficients(index, mask, cos_table, sin_table):
    cosines, sines = [], []
    for top in range(0, index.shape[0], SUBLANES):
        rows = slice(top, top + SUBLANES)
        active = mask[rows] == 1
        cosines.append(jnp.where(active, lookup(index[rows], active, cos_table), 1.0))
        sines.append(jnp.where(active, lookup(index[rows], active, sin_table), 0.0))
    return jnp.concatenate(cosines, axis=0), jnp.concatenate(sines, axis=0)


def tables(angles_ref):
    angle_row = angles_ref[...]
    cos_row = jnp.broadcast_to(jnp.cos(angle_row), (SUBLANES, LANES))
    sin_row = jnp.broadcast_to(jnp.sin(angle_row), (SUBLANES, LANES))
    return cos_row, sin_row


def mirrored_lanes(values):
    width = values.shape[1]
    order = LANES - 1 - lax.broadcasted_iota(jnp.int32, (SUBLANES, LANES), 1)
    rows = []
    for top in range(0, values.shape[0], SUBLANES):
        parts = []
        for start in range(width - LANES, -1, -LANES):
            piece = values[top : top + SUBLANES, start : start + LANES]
            parts.append(jnp.take_along_axis(piece, order, axis=1, mode="promise_in_bounds"))
        rows.append(jnp.concatenate(parts, axis=1))
    return jnp.concatenate(rows, axis=0)


def upward_rows(index_ref, mask_ref, cos_row, sin_row):
    cosines, sines = coefficients(index_ref[...], mask_ref[...], cos_row, sin_row)
    layer = lax.broadcasted_iota(jnp.int32, cosines.shape, 0) // ROWS
    odd = layer % 2 == 1
    return (
        jnp.where(odd, mirrored_lanes(cosines), cosines),
        jnp.where(odd, mirrored_lanes(sines), sines),
    )


def turned(rows_list, table_ref):
    stacked = jnp.concatenate(rows_list, axis=0)
    missing = LANES - stacked.shape[0]
    if missing:
        stacked = jnp.concatenate(
            [stacked, jnp.zeros((missing, stacked.shape[1]), jnp.float32)], axis=0
        )
    for start in range(0, stacked.shape[1], LANES):
        table_ref[start : start + LANES, :] = stacked[:, start : start + LANES].T


def flipped(block):
    order = SUBLANES - 1 - lax.broadcasted_iota(jnp.int32, (SUBLANES, LANES), 0)
    parts = [
        jnp.take_along_axis(block[top : top + SUBLANES], order, axis=0, mode="promise_in_bounds")
        for top in range(block.shape[0] - SUBLANES, -1, -SUBLANES)
    ]
    return jnp.concatenate(parts, axis=0)


def local_kernel(
    angles_ref, hidx_ref, hmask_ref, vidx_ref, vmask_ref, slab_ref, low_ref, high_ref,
    table_ref, first_ref, second_ref,
):
    width = hidx_ref.shape[1]

    @pl.when(pl.program_id(0) == 0)
    def _():
        cos_row, sin_row = tables(angles_ref)
        cosines, sines = coefficients(hidx_ref[...], hmask_ref[...], cos_row, sin_row)
        place = lax.broadcasted_iota(jnp.int32, cosines.shape, 1)
        layer = lax.broadcasted_iota(jnp.int32, cosines.shape, 0) // ROWS
        starts = place % 2 == layer % 2
        lone = (layer == 1) & ((place == 0) | (place == width - 1))
        own_part = jnp.where(starts, cosines, pltpu.roll(cosines, 1, 1))
        other_part = jnp.where(starts, -sines, pltpu.roll(sines, 1, 1))
        up_cos, up_sin = upward_rows(vidx_ref, vmask_ref, cos_row, sin_row)
        turned(
            [jnp.where(lone, 1.0, own_part), jnp.where(lone, 0.0, other_part), up_cos, up_sin],
            table_ref,
        )
        zeros = jnp.zeros((SUBLANES, LANES), jnp.float32)
        for y in range(ROWS):
            first_ref[y, 0:SUBLANES, :] = zeros
            first_ref[y, width + SUBLANES : width + 2 * SUBLANES, :] = zeros

    def column(k, start):
        return jnp.broadcast_to(table_ref[start : start + BLOCK, k : k + 1], (BLOCK, LANES))

    def pair(v, y, start):
        k = 4 * ROWS + v * ROWS + y
        return column(k, start), column(k + LAYERS_UP * ROWS, start)

    odd = lax.broadcasted_iota(jnp.int32, (BLOCK, LANES), 0) % 2 == 1
    for y in range(ROWS):
        for start in range(0, width, BLOCK):
            here = slab_ref[y * width + start : y * width + start + BLOCK, :]
            partner = jnp.where(odd, pltpu.roll(here, 1, 0), pltpu.roll(here, BLOCK - 1, 0))
            first_ref[y, SUBLANES + start : SUBLANES + start + BLOCK, :] = (
                column(y, start) * here + column(2 * ROWS + y, start) * partner
            )
        for start in range(0, width, BLOCK):
            base = SUBLANES + start
            here = first_ref[y, base : base + BLOCK, :]
            partner = jnp.where(
                odd,
                first_ref[y, base + 1 : base + 1 + BLOCK, :],
                first_ref[y, base - 1 : base - 1 + BLOCK, :],
            )
            result = column(ROWS + y, start) * here + column(3 * ROWS + y, start) * partner
            if y % 2 == 0:
                second_ref[y, start : start + BLOCK, :] = result
            else:
                second_ref[y, width - start - BLOCK : width - start, :] = flipped(result)
    for start in range(0, width, BLOCK):
        r0, r1, r2, r3 = (second_ref[y, start : start + BLOCK, :] for y in range(ROWS))
        c, s = pair(0, 0, start)
        r0, r1 = c * r0 - s * r1, s * r0 + c * r1
        c, s = pair(0, 2, start)
        r2, r3 = c * r2 - s * r3, s * r2 + c * r3
        c, s = pair(1, 1, start)
        r1, r2 = c * r1 - s * r2, s * r1 + c * r2
        low_ref[start : start + BLOCK, :] = r0
        low_ref[width + start : width + start + BLOCK, :] = r1
        high_ref[start : start + BLOCK, :] = r2
        high_ref[width + start : width + start + BLOCK, :] = r3


def closing_kernel(
    angles_ref, vidx_ref, vmask_ref, pidx_ref, pmask_ref, nidx_ref, nmask_ref,
    low_ref, high_ref, above_ref, below_ref, trial_ref, *rest,
):
    evolved_ref, keep_ref, give_ref, table_ref, sum_ref = rest[-5:]
    width = vidx_ref.shape[1]
    half = keep_ref.shape[0]

    @pl.when(pl.program_id(0) == 0)
    def _():
        cos_row, sin_row = tables(angles_ref)
        rows_list = []
        for index_ref, mask_ref in ((vidx_ref, vmask_ref), (pidx_ref, pmask_ref), (nidx_ref, nmask_ref)):
            rows_list.extend(upward_rows(index_ref, mask_ref, cos_row, sin_row))
        turned(rows_list, table_ref)

    def column(k, start):
        return jnp.broadcast_to(table_ref[start : start + BLOCK, k : k + 1], (BLOCK, LANES))

    def pair(who, v, y, start):
        k = who * 2 * LAYERS_UP * ROWS + v * ROWS + y
        return column(k, start), column(k + LAYERS_UP * ROWS, start)

    for start in range(0, width, BLOCK):
        near, far = slice(start, start + BLOCK), slice(width + start, width + start + BLOCK)
        r0, r1, r2, r3 = low_ref[near, :], low_ref[far, :], high_ref[near, :], high_ref[far, :]
        n0, n1 = above_ref[near, :], above_ref[far, :]
        p2, p3 = below_ref[near, :], below_ref[far, :]
        c, s = pair(0, 1, 3, start)
        r3, n0 = c * r3 - s * n0, s * r3 + c * n0
        c, s = pair(1, 1, 3, start)
        p3, r0 = c * p3 - s * r0, s * p3 + c * r0
        c, s = pair(0, 2, 0, start)
        r0, r1 = c * r0 - s * r1, s * r0 + c * r1
        c, s = pair(0, 2, 2, start)
        r2, r3 = c * r2 - s * r3, s * r2 + c * r3
        c, s = pair(2, 2, 0, start)
        n0 = c * n0 - s * n1
        c, s = pair(1, 2, 2, start)
        p3 = s * p2 + c * p3
        c, s = pair(0, 3, 1, start)
        r1, r2 = c * r1 - s * r2, s * r1 + c * r2
        c, s = pair(0, 3, 3, start)
        r3 = c * r3 - s * n0
        c, s = pair(1, 3, 3, start)
        r0 = s * p3 + c * r0
        mirror = width - start - BLOCK
        evolved_ref[start : start + BLOCK, :] = r0
        evolved_ref[width + mirror : width + mirror + BLOCK, :] = flipped(r1)
        evolved_ref[2 * width + start : 2 * width + start + BLOCK, :] = r2
        evolved_ref[3 * width + mirror : 3 * width + mirror + BLOCK, :] = flipped(r3)
    sum_ref[...] = lax.dot_general(
        trial_ref[...],
        evolved_ref[...],
        (((0,), (0,)), ((), ())),
        precision=lax.Precision.HIGHEST,
        preferred_element_type=jnp.float32,
    )
    side = lax.axis_index("rows") % 2
    keep_ref[...] = sum_ref[pl.ds(pl.multiple_of(side * half, half), half), :]
    give_ref[...] = sum_ref[pl.ds(pl.multiple_of((1 - side) * half, half), half), :]


def whole(array):
    return pl.BlockSpec(array.shape, lambda i: (0,) * array.ndim)


def params():
    return pltpu.CompilerParams(
        dimension_semantics=("arbitrary",), vmem_limit_bytes=48 * 1024 * 1024
    )


def local_step(angles, hidx, hmask, vidx, vmask, slab, first, count):
    rows = slab.shape[0]
    width = hidx.shape[1]
    small = (angles, hidx, hmask, vidx, vmask)
    half = jax.ShapeDtypeStruct((rows // 2, count * LANES), jnp.float32)
    return pl.pallas_call(
        local_kernel,
        grid=(count,),
        in_specs=[whole(a) for a in small]
        + [pl.BlockSpec((rows, LANES), lambda i: (0, first + i))],
        out_specs=[pl.BlockSpec((rows // 2, LANES), lambda i: (0, i))] * 2,
        out_shape=[half, half],
        scratch_shapes=[
            pltpu.VMEM((width, LANES), jnp.float32),
            pltpu.VMEM((ROWS, width + 2 * SUBLANES, LANES), jnp.float32),
            pltpu.VMEM((ROWS, width, LANES), jnp.float32),
        ],
        compiler_params=params(),
        name="local_step",
        cost_estimate=pl.CostEstimate(
            flops=16 * rows * count * LANES, bytes_accessed=8 * rows * count * LANES, transcendentals=0
        ),
    )(*small, slab)


def closing_step(angles, ups, low, high, above, below, trial, evolved, columns, first, count):
    rows = trial.shape[0]
    wide = trial.shape[1]
    width = ups[0].shape[1]
    small = (angles, *ups)
    tile = pl.BlockSpec((rows // 2, LANES), lambda i: (0, i))
    half = jax.ShapeDtypeStruct((wide // 2, count * LANES), jnp.float32)
    operands = [*small, low, high, above, below, trial]
    in_specs = [whole(a) for a in small] + [tile] * 4 + [whole(trial)]
    aliases = {}
    if evolved is not None:
        aliases = {len(operands): 0}
        operands.append(evolved)
        in_specs.append(pl.BlockSpec(memory_space=pl.ANY))
    return pl.pallas_call(
        closing_kernel,
        grid=(count,),
        in_specs=in_specs,
        out_specs=[
            pl.BlockSpec((rows, LANES), lambda i: (0, first + i)),
            pl.BlockSpec((wide // 2, LANES), lambda i: (0, i)),
            pl.BlockSpec((wide // 2, LANES), lambda i: (0, i)),
        ],
        out_shape=[jax.ShapeDtypeStruct((rows, columns), jnp.float32), half, half],
        scratch_shapes=[
            pltpu.VMEM((width, LANES), jnp.float32),
            pltpu.VMEM((wide, LANES), jnp.float32),
        ],
        input_output_aliases=aliases,
        compiler_params=params(),
        name="closing_step",
        cost_estimate=pl.CostEstimate(
            flops=12 * rows * wide * count * LANES,
            bytes_accessed=12 * rows * count * LANES + 4 * rows * wide,
            transcendentals=0,
        ),
    )(*operands)


def join_kernel(*refs):
    out_ref = refs[-1]
    side = lax.axis_index("rows") % 2
    half = out_ref.shape[0] // 2
    start = 0
    for mine_ref, other_ref in zip(refs[:-1:2], refs[1:-1:2]):
        stop = start + mine_ref.shape[1]
        out_ref[pl.ds(pl.multiple_of(side * half, half), half), start:stop] = mine_ref[...]
        out_ref[pl.ds(pl.multiple_of((1 - side) * half, half), half), start:stop] = other_ref[...]
        start = stop


def join(pieces, wide, columns):
    flat = [a for piece in pieces for a in piece]
    return pl.pallas_call(
        join_kernel,
        in_specs=[pl.BlockSpec(memory_space=pltpu.VMEM)] * len(flat),
        out_specs=pl.BlockSpec(memory_space=pltpu.VMEM),
        out_shape=jax.ShapeDtypeStruct((wide, columns), jnp.float32),
        compiler_params=pltpu.CompilerParams(vmem_limit_bytes=16 * 1024 * 1024),
        name="join",
    )(*flat)


def exchange(block, distances):
    count = lax.axis_size("rows")
    return lax.ppermute(block, "rows", [(i, i ^ distances[i % 2]) for i in range(count)])


def shifted(block, distance):
    count = lax.axis_size("rows")
    return lax.ppermute(block, "rows", [(i, (i + distance) % count) for i in range(count)])


def chip_orders(count):
    bits = []
    bit = 2
    while bit < count:
        bits.append(bit)
        bit *= 2
    return list(zip(bits[1:] + bits[:1], bits))


CHUNKS = (4,)


def per_device(
    orbitals, trial_orbitals, angles, horizontal_index, horizontal_mask, vertical_index, vertical_mask
):
    width = horizontal_index.shape[2]
    columns = orbitals.shape[1]
    wide = trial_orbitals.shape[1]
    angle_row = angles.reshape(1, -1)
    hidx, hmask = (a.reshape(-1, width) for a in (horizontal_index, horizontal_mask))
    vidx, vmask = (a.reshape(-1, width) for a in (vertical_index, vertical_mask))
    ups = (vidx, vmask, shifted(vidx, 1), shifted(vmask, 1), shifted(vidx, -1), shifted(vmask, -1))
    orders = chip_orders(lax.axis_size("rows"))
    evolved = None
    pieces = []
    first = 0
    chunks = []
    for count in CHUNKS:
        low, high = local_step(angle_row, hidx, hmask, vidx, vmask, orbitals, first, count)
        chunks.append((first, count, low, high, shifted(low, -1), shifted(high, 1)))
        first += count
    for first, count, low, high, above, below in chunks:
        evolved, keep, give = closing_step(
            angle_row, ups, low, high, above, below, trial_orbitals, evolved, columns, first, count
        )
        total = keep + exchange(give, (1, 1))
        for distances in orders:
            total = total + exchange(total, distances)
        pieces.append((total, exchange(total, (1, 1))))
    return evolved, join(pieces, wide, columns)


def solution(mesh):
    in_specs = (
        P("rows", "groups"),
        P("rows", "groups"),
        P(),
        P("groups", "rows", None),
        P("groups", "rows", None),
        P("groups", "rows", None),
        P("groups", "rows", None),
    )
    out_specs = (P("rows", "groups"), P("groups", None))
    return jax.shard_map(
        per_device, mesh=mesh, in_specs=in_specs, out_specs=out_specs, check_vma=False
    )
```

```python
import functools

import jax
import jax.numpy as jnp
from jax import lax
from jax.experimental import pallas as pl
from jax.experimental.pallas import tpu as pltpu
from jax.sharding import PartitionSpec as P

LANES = 128
SUBLANES = 8
BLOCK = 64
ROWS = 4
LAYERS_UP = 4


def lookup(index, mask, table):
    parts = []
    for start in range(0, index.shape[1], LANES):
        piece = index[:, start : start + LANES]
        parts.append(jnp.take_along_axis(table, piece, axis=1, mode="promise_in_bounds"))
    return jnp.concatenate(parts, axis=1)


def coefficients(index, mask, cos_table, sin_table):
    cosines, sines = [], []
    for top in range(0, index.shape[0], SUBLANES):
        rows = slice(top, top + SUBLANES)
        active = mask[rows] == 1
        cosines.append(jnp.where(active, lookup(index[rows], active, cos_table), 1.0))
        sines.append(jnp.where(active, lookup(index[rows], active, sin_table), 0.0))
    return jnp.concatenate(cosines, axis=0), jnp.concatenate(sines, axis=0)


def tables(angles_ref):
    angle_row = angles_ref[...]
    cos_row = jnp.broadcast_to(jnp.cos(angle_row), (SUBLANES, LANES))
    sin_row = jnp.broadcast_to(jnp.sin(angle_row), (SUBLANES, LANES))
    return cos_row, sin_row


def mirrored_lanes(values):
    width = values.shape[1]
    order = LANES - 1 - lax.broadcasted_iota(jnp.int32, (SUBLANES, LANES), 1)
    rows = []
    for top in range(0, values.shape[0], SUBLANES):
        parts = []
        for start in range(width - LANES, -1, -LANES):
            piece = values[top : top + SUBLANES, start : start + LANES]
            parts.append(jnp.take_along_axis(piece, order, axis=1, mode="promise_in_bounds"))
        rows.append(jnp.concatenate(parts, axis=1))
    return jnp.concatenate(rows, axis=0)


def upward_rows(index_ref, mask_ref, cos_row, sin_row):
    cosines, sines = coefficients(
        stacked_layers(index_ref), stacked_layers(mask_ref), cos_row, sin_row
    )
    layer = lax.broadcasted_iota(jnp.int32, cosines.shape, 0) // ROWS
    odd = layer % 2 == 1
    return (
        jnp.where(odd, mirrored_lanes(cosines), cosines),
        jnp.where(odd, mirrored_lanes(sines), sines),
    )


def turned(rows_list, table_ref):
    stacked = jnp.concatenate(rows_list, axis=0)
    missing = LANES - stacked.shape[0]
    if missing:
        stacked = jnp.concatenate(
            [stacked, jnp.zeros((missing, stacked.shape[1]), jnp.float32)], axis=0
        )
    for start in range(0, stacked.shape[1], LANES):
        table_ref[start : start + LANES, :] = stacked[:, start : start + LANES].T


def flipped(block):
    order = SUBLANES - 1 - lax.broadcasted_iota(jnp.int32, (SUBLANES, LANES), 0)
    parts = [
        jnp.take_along_axis(block[top : top + SUBLANES], order, axis=0, mode="promise_in_bounds")
        for top in range(block.shape[0] - SUBLANES, -1, -SUBLANES)
    ]
    return jnp.concatenate(parts, axis=0)


CHUNK = 128


def stacked_layers(ref):
    return jnp.concatenate([ref[layer] for layer in range(ref.shape[0])], axis=0)


def local_kernel(first, column_block, width, *refs):
    if first:
        angles_ref, hidx_ref, hmask_ref, vidx_ref, vmask_ref, slab_ref = refs[:6]
        low_ref, high_ref, table_ref = refs[6:9]
    else:
        table_ref, slab_ref, low_ref, high_ref = refs[:4]
    raw_ref, first_ref, second_ref, sems = refs[-4:]
    lanes = pl.ds(column_block * CHUNK, CHUNK)
    copies = [
        pltpu.make_async_copy(
            slab_ref.at[pl.ds(y * width, width), lanes], raw_ref.at[y], sems.at[y]
        )
        for y in range(ROWS)
    ]
    for copy in copies:
        copy.start()
    if first:
        cos_row, sin_row = tables(angles_ref)
        cosines, sines = coefficients(
            stacked_layers(hidx_ref), stacked_layers(hmask_ref), cos_row, sin_row
        )
        place = lax.broadcasted_iota(jnp.int32, cosines.shape, 1)
        layer = lax.broadcasted_iota(jnp.int32, cosines.shape, 0) // ROWS
        starts = place % 2 == layer % 2
        lone = (layer == 1) & ((place == 0) | (place == width - 1))
        own_part = jnp.where(starts, cosines, pltpu.roll(cosines, 1, 1))
        other_part = jnp.where(starts, -sines, pltpu.roll(sines, 1, 1))
        up_cos, up_sin = upward_rows(vidx_ref, vmask_ref, cos_row, sin_row)
        turned(
            [jnp.where(lone, 1.0, own_part), jnp.where(lone, 0.0, other_part), up_cos, up_sin],
            table_ref,
        )
        to_next = jnp.concatenate(
            [part[k : k + 1] for part in (up_cos, up_sin) for k in (7, 10, 15, 15)], axis=0
        )
        to_last = jnp.concatenate(
            [part[k : k + 1] for part in (up_cos, up_sin) for k in (8, 8, 8, 8)], axis=0
        )
        for start in range(0, width, LANES):
            rows = slice(2 * width + start // LANES * SUBLANES, 2 * width + (start // LANES + 1) * SUBLANES)
            high_ref[rows, :] = to_next[:, start : start + LANES]
            low_ref[rows, :] = to_last[:, start : start + LANES]
    zeros = jnp.zeros((SUBLANES, LANES), jnp.float32)
    for y in range(ROWS):
        first_ref[y, 0:SUBLANES, :] = zeros
        first_ref[y, width + SUBLANES : width + 2 * SUBLANES, :] = zeros

    def column(k, start):
        return jnp.broadcast_to(table_ref[start : start + BLOCK, k : k + 1], (BLOCK, LANES))

    def pair(v, y, start):
        k = 4 * ROWS + v * ROWS + y
        return column(k, start), column(k + LAYERS_UP * ROWS, start)

    odd = lax.broadcasted_iota(jnp.int32, (BLOCK, LANES), 0) % 2 == 1
    for y in range(ROWS):
        copies[y].wait()
        for start in range(0, width, BLOCK):
            here = raw_ref[y, start : start + BLOCK, :]
            partner = jnp.where(odd, pltpu.roll(here, 1, 0), pltpu.roll(here, BLOCK - 1, 0))
            first_ref[y, SUBLANES + start : SUBLANES + start + BLOCK, :] = (
                column(y, start) * here + column(2 * ROWS + y, start) * partner
            )
        for start in range(0, width, BLOCK):
            base = SUBLANES + start
            here = first_ref[y, base : base + BLOCK, :]
            partner = jnp.where(
                odd,
                first_ref[y, base + 1 : base + 1 + BLOCK, :],
                first_ref[y, base - 1 : base - 1 + BLOCK, :],
            )
            result = column(ROWS + y, start) * here + column(3 * ROWS + y, start) * partner
            if y % 2 == 0:
                second_ref[y, start : start + BLOCK, :] = result
            else:
                second_ref[y, width - start - BLOCK : width - start, :] = flipped(result)
    for start in range(0, width, BLOCK):
        r0, r1, r2, r3 = (second_ref[y, start : start + BLOCK, :] for y in range(ROWS))
        c, s = pair(0, 0, start)
        r0, r1 = c * r0 - s * r1, s * r0 + c * r1
        c, s = pair(0, 2, start)
        r2, r3 = c * r2 - s * r3, s * r2 + c * r3
        c, s = pair(1, 1, start)
        r1, r2 = c * r1 - s * r2, s * r1 + c * r2
        low_ref[start : start + BLOCK, :] = r0
        low_ref[width + start : width + start + BLOCK, :] = r1
        high_ref[start : start + BLOCK, :] = r2
        high_ref[width + start : width + start + BLOCK, :] = r3


def closing_kernel(first, column_block, width, *refs):
    table_ref, low_ref, high_ref, above_ref, below_ref, trial_ref = refs[:6]
    if first:
        evolved_ref, keep_ref, give_ref, full_ref = refs[6:10]
    else:
        full_ref = table_ref
        evolved_ref, keep_ref, give_ref = refs[7:10]
    out_ref, parts_ref, sum_ref, sem = refs[-4:]
    half = keep_ref.shape[0]
    wide = 2 * half
    base = 4 * ROWS + 2 * LAYERS_UP * ROWS
    if first:
        for start in range(0, width, LANES):
            rows = slice(2 * width + start // LANES * SUBLANES, 2 * width + (start // LANES + 1) * SUBLANES)
            extra = jnp.concatenate(
                [below_ref[rows, :], above_ref[rows, :], jnp.zeros((LANES - 2 * SUBLANES, LANES), jnp.float32)],
                axis=0,
            ).T
            near = slice(start, start + LANES)
            full_ref[near, 0:base] = table_ref[near, 0:base]
            full_ref[near, base : base + 2 * SUBLANES] = extra[:, 0 : 2 * SUBLANES]

    def column(k, start):
        return jnp.broadcast_to(full_ref[start : start + BLOCK, k : k + 1], (BLOCK, LANES))

    def pair(v, y, start):
        k = 4 * ROWS + v * ROWS + y
        return column(k, start), column(k + LAYERS_UP * ROWS, start)

    def outer(k, start):
        return column(base + k, start), column(base + k + 4, start)

    for start in range(0, width, BLOCK):
        near, far = slice(start, start + BLOCK), slice(width + start, width + start + BLOCK)
        r0, r1, r2, r3 = low_ref[near, :], low_ref[far, :], high_ref[near, :], high_ref[far, :]
        n0, n1 = above_ref[near, :], above_ref[far, :]
        p2, p3 = below_ref[near, :], below_ref[far, :]
        c, s = pair(1, 3, start)
        r3, n0 = c * r3 - s * n0, s * r3 + c * n0
        c, s = outer(0, start)
        p3, r0 = c * p3 - s * r0, s * p3 + c * r0
        c, s = pair(2, 0, start)
        r0, r1 = c * r0 - s * r1, s * r0 + c * r1
        c, s = pair(2, 2, start)
        r2, r3 = c * r2 - s * r3, s * r2 + c * r3
        c, s = outer(SUBLANES, start)
        n0 = c * n0 - s * n1
        c, s = outer(1, start)
        p3 = s * p2 + c * p3
        c, s = pair(3, 1, start)
        r1, r2 = c * r1 - s * r2, s * r1 + c * r2
        c, s = pair(3, 3, start)
        r3 = c * r3 - s * n0
        c, s = outer(2, start)
        r0 = s * p3 + c * r0
        mirror = width - start - BLOCK
        for top, value in (
            (start, r0),
            (width + mirror, flipped(r1)),
            (2 * width + start, r2),
            (3 * width + mirror, flipped(r3)),
        ):
            rows = slice(top, top + BLOCK)
            out_ref[rows, :] = value
            upper = value.astype(jnp.bfloat16)
            parts_ref[rows, 0:CHUNK] = upper
            parts_ref[rows, CHUNK : 2 * CHUNK] = (value - upper.astype(jnp.float32)).astype(jnp.bfloat16)
    copy = pltpu.make_async_copy(
        out_ref, evolved_ref.at[:, pl.ds(column_block * CHUNK, CHUNK)], sem
    )
    copy.start()
    product = jnp.dot(trial_ref[...], parts_ref[...], preferred_element_type=jnp.float32)
    product = product[:, 0:CHUNK] + product[:, CHUNK : 2 * CHUNK]
    sum_ref[...] = product[0:wide] + product[wide : 2 * wide]
    side = lax.axis_index("rows") % 2
    keep_ref[...] = sum_ref[pl.ds(pl.multiple_of(side * half, half), half), :]
    give_ref[...] = sum_ref[pl.ds(pl.multiple_of((1 - side) * half, half), half), :]
    copy.wait()


VMEM = pl.BlockSpec(memory_space=pltpu.VMEM)
ANY = pl.BlockSpec(memory_space=pl.ANY)


def params(mib):
    return pltpu.CompilerParams(vmem_limit_bytes=mib * 1024 * 1024)


def cost(flops, moved):
    return pl.CostEstimate(flops=flops, bytes_accessed=moved, transcendentals=0)


def local_step(small, table, slab, width, block):
    rows = slab.shape[0]
    first = table is None
    extra = width // LANES * SUBLANES if first else 0
    half = jax.ShapeDtypeStruct((rows // 2 + extra, CHUNK), jnp.float32)
    operands = [*small, slab] if first else [table, slab]
    out_shape = [half, half]
    if first:
        out_shape.append(jax.ShapeDtypeStruct((width, LANES), jnp.float32))
    return pl.pallas_call(
        functools.partial(local_kernel, first, block, width),
        in_specs=[VMEM] * (len(operands) - 1) + [ANY],
        out_specs=[VMEM] * len(out_shape),
        out_shape=out_shape,
        scratch_shapes=[
            pltpu.VMEM((ROWS, width, LANES), jnp.float32),
            pltpu.VMEM((ROWS, width + 2 * SUBLANES, LANES), jnp.float32),
            pltpu.VMEM((ROWS, width, LANES), jnp.float32),
            pltpu.SemaphoreType.DMA((ROWS,)),
        ],
        compiler_params=params(16),
        name="local_step",
        cost_estimate=cost(16 * rows * CHUNK, 8 * rows * CHUNK),
    )(*operands)


def trial_kernel(trial_ref, late_ref, parts_ref):
    wide = trial_ref.shape[1]
    turned_block = trial_ref[...].T
    upper = turned_block.astype(jnp.bfloat16)
    parts_ref[0:wide, :] = upper
    parts_ref[wide : 2 * wide, :] = (turned_block - upper.astype(jnp.float32)).astype(jnp.bfloat16)


def trial_step(trial, late):
    rows, wide = trial.shape
    tall = 512
    return pl.pallas_call(
        trial_kernel,
        grid=(rows // tall,),
        in_specs=[pl.BlockSpec((tall, wide), lambda i: (i, 0)), ANY],
        out_specs=pl.BlockSpec((2 * wide, tall), lambda i: (0, i)),
        out_shape=jax.ShapeDtypeStruct((2 * wide, rows), jnp.bfloat16),
        compiler_params=params(16),
        name="trial_step",
        cost_estimate=cost(4 * rows * wide, 8 * rows * wide),
    )(trial, late)


def closing_step(table, low, high, above, below, trial, evolved, width, columns, block):
    wide = trial.shape[0] // 2
    rows = trial.shape[1]
    first = evolved is None
    half = jax.ShapeDtypeStruct((wide // 2, CHUNK), jnp.float32)
    operands = [table, low, high, above, below, trial]
    in_specs = [VMEM] * 6
    out_shape = [jax.ShapeDtypeStruct((rows, columns), jnp.float32), half, half]
    out_specs = [ANY, VMEM, VMEM]
    aliases = {}
    if first:
        out_shape.append(jax.ShapeDtypeStruct(table.shape, jnp.float32))
        out_specs.append(VMEM)
    else:
        aliases = {len(operands): 0}
        operands.append(evolved)
        in_specs.append(ANY)
    return pl.pallas_call(
        functools.partial(closing_kernel, first, block, width),
        in_specs=in_specs,
        out_specs=out_specs,
        out_shape=out_shape,
        scratch_shapes=[
            pltpu.VMEM((rows, CHUNK), jnp.float32),
            pltpu.VMEM((rows, 2 * CHUNK), jnp.bfloat16),
            pltpu.VMEM((wide, CHUNK), jnp.float32),
            pltpu.SemaphoreType.DMA,
        ],
        input_output_aliases=aliases,
        compiler_params=params(24),
        name="closing_step",
        cost_estimate=cost(8 * rows * wide * CHUNK, 12 * rows * CHUNK),
    )(*operands)


def join_kernel(*refs):
    out_ref = refs[-1]
    side = lax.axis_index("rows") % 2
    half = out_ref.shape[0] // 2
    start = 0
    for mine_ref, other_ref in zip(refs[:-1:2], refs[1:-1:2]):
        stop = start + mine_ref.shape[1]
        out_ref[pl.ds(pl.multiple_of(side * half, half), half), start:stop] = mine_ref[...]
        out_ref[pl.ds(pl.multiple_of((1 - side) * half, half), half), start:stop] = other_ref[...]
        start = stop


def join(pieces, wide, columns):
    flat = [a for piece in pieces for a in piece]
    return pl.pallas_call(
        join_kernel,
        in_specs=[pl.BlockSpec(memory_space=pltpu.VMEM)] * len(flat),
        out_specs=pl.BlockSpec(memory_space=pltpu.VMEM),
        out_shape=jax.ShapeDtypeStruct((wide, columns), jnp.float32),
        compiler_params=pltpu.CompilerParams(vmem_limit_bytes=16 * 1024 * 1024),
        name="join",
    )(*flat)


def exchange(block, distances):
    count = lax.axis_size("rows")
    return lax.ppermute(block, "rows", [(i, i ^ distances[i % 2]) for i in range(count)])


def shifted(block, distance):
    count = lax.axis_size("rows")
    return lax.ppermute(block, "rows", [(i, (i + distance) % count) for i in range(count)])


def chip_orders(count):
    bits = []
    bit = 2
    while bit < count:
        bits.append(bit)
        bit *= 2
    return list(zip(bits[1:] + bits[:1], bits))


def per_device(
    orbitals, trial_orbitals, angles, horizontal_index, horizontal_mask, vertical_index, vertical_mask
):
    width = horizontal_index.shape[2]
    columns = orbitals.shape[1]
    wide = trial_orbitals.shape[1]
    small = (angles.reshape(1, -1), horizontal_index, horizontal_mask, vertical_index, vertical_mask)
    orders = chip_orders(lax.axis_size("rows"))
    blocks = range(columns // CHUNK)
    table = None
    chunks = []
    for block in blocks:
        low, high, *made = local_step(small, table, orbitals, width, block)
        table = made[0] if made else table
        chunks.append((low, high, shifted(low, -1), shifted(high, 1)))
    trial = trial_step(trial_orbitals, low)
    evolved = None
    pieces = []
    for block in blocks:
        evolved, keep, give, *made = closing_step(
            table, *chunks[block], trial, evolved, width, columns, block
        )
        table = made[0] if made else table
        total = keep + exchange(give, (1, 1))
        for distances in orders:
            total = total + exchange(total, distances)
        pieces.append((total, exchange(total, (1, 1))))
    return evolved, join(pieces, wide, columns)


def solution(mesh):
    in_specs = (
        P("rows", "groups"),
        P("rows", "groups"),
        P(),
        P("groups", "rows", None),
        P("groups", "rows", None),
        P("groups", "rows", None),
        P("groups", "rows", None),
    )
    out_specs = (P("rows", "groups"), P("groups", None))
    return jax.shard_map(
        per_device, mesh=mesh, in_specs=in_specs, out_specs=out_specs, check_vma=False
    )
```
